32 devices in a mesh: blk: 8 (over z, x), aux: 4 (over y, core).
Axes of the slice: x: 2, y: 2, z: 4, core: 2. Of those that a mesh axis runs over, the one named last changes fastest.
Arguments:
- half_ints: bfloat16 [32, 1536, 384], P('blk', 'aux'), may hold values from -0.625 to 0.625
- metric_inv: bfloat16 [1536, 1536], P('aux'), may hold values from -1 to 2, as said below
- occ_energy: float32 [32], replicated, may hold values from -2 to -0.3
- vir_energy: float32 [384], replicated, may hold values from 0.3 to 3
Outputs:
- gamma: bfloat16 [32, 1536, 384], P('blk', 'aux')
The draws below stay inside these ranges and needn't reach their ends.
Inputs may be any that keep to these rules, and one draw needn't show every extreme that they name: metric_inv is lower triangular (zero where Q > P) with a positive diagonal.
All inputs are finite; a program needn't handle non-finite values.
Results may differ from the reference program's by a relative error of at most 0.0058.
Values may be sent and summed in bfloat16 or wider, within the bound.
A program may use at most 64 MiB of HBM per device.

```python
import math
import jax
import jax.numpy as jnp
from jax import lax

VIR = 384
NAUX = 1536
OCC_SUB = 1
CYCLE = 4
NOCC = 32
N_AUX = 4


def draw_metric_inv(key, part):
    first_key, second_key = jax.random.split(key)
    row_index = lax.broadcasted_iota(jnp.int32, (NAUX, NAUX), 0)
    col_index = lax.broadcasted_iota(jnp.int32, (NAUX, NAUX), 1)
    lower_part = jnp.clip(jax.random.normal(first_key, (NAUX, NAUX), jnp.float32), -4.0, 4.0) * 0.8
    lower_part = lower_part * NAUX ** (-0.5)
    diagonal = jnp.exp(jax.random.uniform(second_key, (NAUX,), jnp.float32, math.log(0.5), math.log(2.0)))
    lower_part = jnp.where(row_index > col_index, lower_part, 0.0)
    return (lower_part + jnp.where(row_index == col_index, diagonal[None, :], 0.0)).astype(jnp.bfloat16)


def level_of(own_key, shape, shards, low, high):
    level = 1.0
    for dim, shards_of in shards:
        draws = jax.random.uniform(jax.random.fold_in(jax.random.fold_in(own_key, 6), dim), (shards_of,), jnp.float32, low / len(shards), high / len(shards))
        level = level * jnp.repeat(jnp.exp(draws), shape[dim] // shards_of).reshape((-1,) + (1,) * (len(shape) - 1 - dim))
    return level


def normal_values(rng, extent, width, bound, cuts=(), held_as=jnp.bfloat16):
    values = jax.random.normal(rng, extent, jnp.float32) * width
    if len(cuts) > 0:
        values = level_of(rng, extent, cuts, -0.22, 0.18) * values
    return jnp.clip(values, min=-bound, max=bound).astype(held_as)


def setup_inputs(seed: int = 0) -> dict:
    key_list = jax.random.split(jax.random.key(seed), 5)
    return {
        "half_ints": normal_values(key_list[0], (NOCC, NAUX, VIR), 0.1, 0.625, ((0, 8), (1, 4))),
        "metric_inv": draw_metric_inv(jax.random.fold_in(key_list[4], 71), 0),
        "occ_energy": jnp.clip(jax.random.uniform(key_list[2], (NOCC,), jnp.float32, -2.0, -0.3), -2.0, -0.3),
        "vir_energy": jnp.clip(jax.random.uniform(key_list[3], (VIR,), jnp.float32, 0.3, 3.0), 0.3, 3.0),
    }


def reference(half_ints, metric_inv, occ_energy, vir_energy):
    unit_count = NOCC // OCC_SUB
    metric_f32 = metric_inv.astype(jnp.float32)

    def fit_unit(occ_block):
        return jnp.einsum("pq,upa->uqa", metric_f32, occ_block.astype(jnp.float32)).astype(jnp.bfloat16)

    fitted = lax.map(fit_unit, half_ints.reshape(unit_count, OCC_SUB, NAUX, VIR))
    energies = occ_energy.astype(jnp.float32).reshape(unit_count, OCC_SUB)
    virtuals = vir_energy.astype(jnp.float32)

    def density_unit(unit_index):
        own_block = fitted[unit_index].astype(jnp.float32)
        own_energy = energies[unit_index]
        density_acc = jnp.zeros((OCC_SUB, NAUX, VIR), jnp.float32)
        for cycle_step in range(CYCLE):
            partner_index = ((unit_index - cycle_step * N_AUX) % unit_count).astype(jnp.int32)
            partner = fitted[partner_index].astype(jnp.float32)
            partner_energy = energies[partner_index]
            pair_ints = jnp.einsum("uqa,vqb->uvab", own_block, partner)
            energy_gap = (own_energy[:, None, None, None] + partner_energy[None, :, None, None]
                          - virtuals[None, None, :, None] - virtuals[None, None, None, :])
            amplitude = ((2.0 * pair_ints - jnp.swapaxes(pair_ints, 2, 3)) / energy_gap).astype(jnp.bfloat16)
            density_acc = density_acc + jnp.einsum("uvab,vqb->uqa", amplitude.astype(jnp.float32), partner)
        density_fit = density_acc.astype(jnp.bfloat16)
        return jnp.einsum("pq,uqa->upa", metric_f32, density_fit.astype(jnp.float32)).astype(jnp.bfloat16)

    gamma = lax.map(density_unit, jnp.arange(unit_count, dtype=jnp.int32))
    return gamma.reshape(NOCC, NAUX, VIR)
```

```python
import functools

import jax
import jax.numpy as jnp
from jax import lax
from jax.experimental import pallas as pl
from jax.experimental.pallas import tpu as pltpu
from jax.sharding import PartitionSpec as P

CYCLE = 4
MESH = pl.DeviceIdType.MESH


def kernel(
    blocks, groups, tile,
    ints_ref, metric_ref, occ_ref, vir_ref,
    out_ref,
    ints, metric, metric_t, fit, fit_t, gap, dens, dens_b, gam,
    h_send, h_recv, z_send, c_send, f_send, w_send, ring_recv,
    m1_send, m1_recv, m2_send, m2_recv, m3_send, m3_recv, own_sem, g_send, g_recv,
):
    shard = ints_ref.shape[1]
    half = shard // 2
    naux = metric_ref.shape[1]
    vir = ints_ref.shape[2]
    tiles = naux // tile
    pairs = groups // 2
    b, g = lax.axis_index("blk"), lax.axis_index("aux")
    x, core, h = b % 2, g % 2, g // 2
    plane, mate, ahead = b - x, g + 1 - 2 * core, (b + 2) % blocks
    across = b + 1 - 2 * x
    own_b, own_c = plane + core, g - core + x

    def rows(p):
        return pl.ds(pl.multiple_of(p * shard, shard), shard)

    def halves(p, which):
        return pl.ds(pl.multiple_of(p * shard + which * half, half), half)

    def width(hv):
        return min(naux, -(-2 * shard * (hv + 1) // tile) * tile)

    def remote(src, dst, send, recv, device):
        return pltpu.make_async_remote_copy(
            src_ref=src, dst_ref=dst, send_sem=send, recv_sem=recv,
            device_id=device, device_id_type=MESH,
        )

    def landed(dst, recv):
        pltpu.make_async_copy(dst, dst, recv).wait()

    barrier = pltpu.get_barrier_semaphore()
    for xx in range(2):
        for gg in range(groups):
            @pl.when((plane + xx != b) | (gg != g))
            def _():
                pl.semaphore_signal(barrier, inc=1, device_id=(plane + xx, gg), device_id_type=MESH)
    for bb in (ahead, (b + blocks - 2) % blocks):
        for gg in (g, mate):
            pl.semaphore_signal(barrier, inc=1, device_id=(bb, gg), device_id_type=MESH)
    pl.semaphore_wait(barrier, 2 * groups + 3)

    def ints_copy(c):
        return remote(
            ints_ref.at[c], ints.at[0, rows(g)], h_send.at[c], h_recv.at[g],
            (plane + c % 2, c - c % 2 + x),
        )

    def to_self(c):
        return (core == x) & (c == own_c)

    order = [(2 * ((h + r) % pairs) + par) for r in range(pairs) for par in range(2)]
    for c in order:
        @pl.when(jnp.logical_not(to_self(c)))
        def _():
            ints_copy(c).start()

        @pl.when(to_self(c))
        def _():
            pltpu.make_async_copy(ints_ref.at[c], ints.at[0, rows(g)], h_recv.at[g]).start()

    own_metric = pltpu.make_async_copy(metric_ref, metric.at[rows(g)], own_sem)
    own_metric.start()

    def m1_copy(hv, r):
        return remote(
            metric_ref.at[pl.ds(pl.multiple_of(x * half, half), half), pl.ds(0, width(hv))],
            metric.at[halves(g, x), pl.ds(0, width(hv))],
            m1_send.at[r], m1_recv.at[hv],
            (b, 2 * ((h + r) % pairs) + core),
        )

    def m3_own(hv):
        return remote(
            metric_ref.at[:, pl.ds(0, width(hv))], metric.at[rows(g), pl.ds(0, width(hv))],
            m3_send.at[hv], m3_recv.at[hv], (b, mate),
        )

    def m2_copy(hv):
        piece = metric.at[halves(2 * hv + core, x), pl.ds(0, width(hv))]
        return remote(piece, piece, m2_send.at[hv], m2_recv.at[hv], (across, g))

    def m3_copy(hv):
        piece = metric.at[rows(2 * hv + core), pl.ds(0, width(hv))]
        return remote(piece, piece, m3_send.at[hv], m3_recv.at[hv], (b, mate))

    for hv in range(pairs):
        @pl.when(h == hv)
        def _():
            for r in range(1, pairs):
                m1_copy(hv, r).start()
            m3_own(hv).start()

    def z_copy(p):
        return remote(ints.at[0, rows(p)], ints.at[2, rows(p)], z_send.at[p], ring_recv.at[2, p], (ahead, g))

    def c_copy(p):
        return remote(ints.at[0, rows(p)], ints.at[1, rows(p)], c_send.at[p], ring_recv.at[1, p], (b, mate))

    def f_copy(p, role):
        return remote(ints.at[2, rows(p)], ints.at[role, rows(p)], f_send.at[p], ring_recv.at[role, p], (b, mate))

    def w_copy(p):
        return remote(ints.at[2, rows(p)], ints.at[3, rows(p)], w_send.at[p], ring_recv.at[3, p], (ahead, mate))

    for p in order:
        landed(ints.at[0, rows(p)], h_recv.at[p])
        z_copy(p).start()

        @pl.when(core == 0)
        def _():
            c_copy(p).start()

    for hv in range(pairs):
        @pl.when(h != hv)
        def _():
            landed(metric.at[halves(2 * hv + core, x), pl.ds(0, width(hv))], m1_recv.at[hv])
            m2_copy(hv).start()
    for hv in range(pairs):
        @pl.when(h != hv)
        def _():
            landed(metric.at[halves(2 * hv + core, 1 - x), pl.ds(0, width(hv))], m2_recv.at[hv])
            m3_copy(hv).start()

    for p in order:
        landed(ints.at[2, rows(p)], ring_recv.at[2, p])

        @pl.when(core == 1)
        def _():
            w_copy(p).start()
            f_copy(p, 1).start()

        @pl.when(core == 0)
        def _():
            f_copy(p, 3).start()

    own_metric.wait()
    for hv in range(pairs):
        landed(metric.at[rows(2 * hv + 1 - core), pl.ds(0, width(hv))], m3_recv.at[hv])

    levels = jnp.broadcast_to(vir_ref[...], (vir, vir))
    gap[...] = levels + levels.T

    def span(q):
        return pl.ds(pl.multiple_of(q * tile, tile), tile)

    @pl.loop(0, tiles)
    def _(p):
        @pl.loop(0, p + 1)
        def _(q):
            metric_t[span(q), span(p)] = metric[span(p), span(q)].T

    dens[...] = jnp.zeros_like(dens)
    own_energy = occ_ref[own_b * groups + own_c]

    @pl.loop(0, CYCLE)
    def _(k):
        role = (k % 2) * 2 + k // 2

        @pl.when(role % 2 == 1)
        def _():
            for p in range(groups):
                landed(ints.at[role, rows(p)], ring_recv.at[role, p])

        for q in range(tiles):
            low = q * tile
            fit[low:low + tile, :] = jnp.dot(
                metric_t[low:low + tile, low:], ints[role, low:, :],
                preferred_element_type=jnp.float32,
            ).astype(fit.dtype)

        @pl.when(k == 0)
        def _():
            @pl.loop(0, tiles)
            def _(q):
                fit_t[:, span(q)] = fit[span(q), :].T

        pair = jnp.dot(fit_t[...], fit[...], preferred_element_type=jnp.float32)
        energy = own_energy + occ_ref[(own_b + blocks - role) % blocks * groups + own_c]
        amplitude_t = ((2.0 * pair.T - pair) / (energy - gap[...])).astype(fit.dtype)

        @pl.loop(0, tiles)
        def _(q):
            dens[span(q), :] += jnp.dot(fit[span(q), :], amplitude_t, preferred_element_type=jnp.float32)

    dens_b[...] = dens[...].astype(dens_b.dtype)

    def g_copy(p):
        return remote(gam.at[rows(p)], out_ref.at[own_c], g_send.at[p], g_recv.at[own_c], (own_b, p))

    def g_self(p):
        return (core == x) & (g == p)

    for t in range(tiles):
        low = t * tile
        gam[low:low + tile, :] = jnp.dot(
            metric[low:low + tile, :low + tile], dens_b[:low + tile, :],
            preferred_element_type=jnp.float32,
        ).astype(gam.dtype)
        for p in range(low // shard, (low + tile) // shard):
            @pl.when(jnp.logical_not(g_self(p)))
            def _():
                g_copy(p).start()

            @pl.when(g_self(p))
            def _():
                pltpu.make_async_copy(gam.at[rows(p)], out_ref.at[own_c], g_recv.at[own_c]).start()

    for c in range(groups):
        @pl.when(jnp.logical_not(to_self(c)))
        def _():
            ints_copy(c).wait_send()
        z_copy(c).wait_send()

        @pl.when(core == 0)
        def _():
            c_copy(c).wait_send()
        f_copy(c, 1).wait_send()

        @pl.when(core == 1)
        def _():
            w_copy(c).wait_send()

        @pl.when(jnp.logical_not(g_self(c)))
        def _():
            g_copy(c).wait_send()
    for hv in range(pairs):
        @pl.when(h == hv)
        def _():
            for r in range(1, pairs):
                m1_copy(hv, r).wait_send()
            m3_own(hv).wait_send()

        @pl.when(h != hv)
        def _():
            m2_copy(hv).wait_send()
            m3_copy(hv).wait_send()
    for c in range(groups):
        landed(out_ref.at[c], g_recv.at[c])


def local(half_ints, metric_inv, occ_energy, vir_energy):
    groups, blocks = lax.axis_size("aux"), lax.axis_size("blk")
    shard, vir = half_ints.shape[1:]
    naux = metric_inv.shape[1]
    tile = shard if shard % 128 == 0 else naux // 4
    pairs = groups // 2
    dma = pltpu.SemaphoreType.DMA
    return pl.pallas_call(
        functools.partial(kernel, blocks, groups, tile),
        out_shape=jax.ShapeDtypeStruct(half_ints.shape, jnp.bfloat16),
        in_specs=[
            pl.BlockSpec(memory_space=pl.ANY),
            pl.BlockSpec(memory_space=pl.ANY),
            pl.BlockSpec(memory_space=pltpu.SMEM),
            pl.BlockSpec(memory_space=pltpu.VMEM),
        ],
        out_specs=pl.BlockSpec(memory_space=pl.ANY),
        scratch_shapes=[
            pltpu.VMEM((CYCLE, naux, vir), jnp.bfloat16),
            pltpu.VMEM((naux, naux), jnp.bfloat16),
            pltpu.VMEM((naux, naux), jnp.bfloat16),
            pltpu.VMEM((naux, vir), jnp.bfloat16),
            pltpu.VMEM((vir, naux), jnp.bfloat16),
            pltpu.VMEM((vir, vir), jnp.float32),
            pltpu.VMEM((naux, vir), jnp.float32),
            pltpu.VMEM((naux, vir), jnp.bfloat16),
            pltpu.VMEM((naux, vir), jnp.bfloat16),
            dma((groups,)), dma((groups,)), dma((groups,)), dma((groups,)), dma((groups,)),
            dma((groups,)), dma((CYCLE, groups)),
            dma((pairs,)), dma((pairs,)), dma((pairs,)), dma((pairs,)), dma((pairs,)), dma((pairs,)),
            dma(()), dma((groups,)), dma((groups,)),
        ],
        compiler_params=pltpu.CompilerParams(
            collective_id=0, has_side_effects=True, vmem_limit_bytes=56 * 2**20
        ),
    )(half_ints, metric_inv, occ_energy, vir_energy[None, :])


def solution(mesh):
    placed = (P("blk", "aux", None), P("aux", None), P(), P())
    return jax.shard_map(
        local, mesh=mesh, in_specs=placed, out_specs=P("blk", "aux", None), check_vma=False
    )
```

```python
import functools

import jax
import jax.numpy as jnp
from jax import lax
from jax.experimental import pallas as pl
from jax.experimental.pallas import tpu as pltpu
from jax.sharding import PartitionSpec as P

CYCLE = 4
MESH = pl.DeviceIdType.MESH


def kernel(
    blocks, groups, tile,
    ints_ref, metric_ref, occ_ref, vir_ref,
    out_ref,
    ints, metric, metric_t, fit, fit_t, gap, dens, dens_b, gam,
    h_send, h_recv, z_send, c_send, f_send, w_send, ring_recv,
    m1_send, m1_recv, m2_send, m2_recv, m3_send, m3_recv, own_sem, g_send, g_recv,
):
    shard = ints_ref.shape[1]
    half = shard // 2
    parts = 4 if half % 64 == 0 else 1
    part = half // parts
    naux = metric_ref.shape[1]
    vir = ints_ref.shape[2]
    tiles = naux // tile
    pairs = groups // 2
    b, g = lax.axis_index("blk"), lax.axis_index("aux")
    x, core, h = b % 2, g % 2, g // 2
    plane, mate, ahead = b - x, g + 1 - 2 * core, (b + 2) % blocks
    across = b + 1 - 2 * x
    own_b, own_c = plane + core, g - core + x

    def rows(p):
        return pl.ds(pl.multiple_of(p * shard, shard), shard)

    def slab(p, which, n):
        return pl.ds(pl.multiple_of(p * shard + which * half + n * part, part), part)

    def width(hv):
        return min(naux, -(-2 * shard * (hv + 1) // tile) * tile)

    def remote(src, dst, send, recv, device):
        return pltpu.make_async_remote_copy(
            src_ref=src, dst_ref=dst, send_sem=send, recv_sem=recv,
            device_id=device, device_id_type=MESH,
        )

    def landed(dst, recv):
        pltpu.make_async_copy(dst, dst, recv).wait()

    barrier = pltpu.get_barrier_semaphore()
    for xx in range(2):
        for gg in range(groups):
            @pl.when((plane + xx != b) | (gg != g))
            def _():
                pl.semaphore_signal(barrier, inc=1, device_id=(plane + xx, gg), device_id_type=MESH)
    for bb in (ahead, (b + blocks - 2) % blocks):
        for gg in (g, mate):
            pl.semaphore_signal(barrier, inc=1, device_id=(bb, gg), device_id_type=MESH)
    pl.semaphore_wait(barrier, 2 * groups + 3)

    def ints_copy(c):
        return remote(
            ints_ref.at[c], ints.at[0, rows(g)], h_send.at[c], h_recv.at[g],
            (plane + c % 2, c - c % 2 + x),
        )

    def to_self(c):
        return (core == x) & (c == own_c)

    order = [(2 * ((h + r) % pairs) + par) for r in range(pairs) for par in range(2)]
    own_metric = pltpu.make_async_copy(metric_ref, metric.at[rows(g)], own_sem)
    own_metric.start()

    def m1_copy(hv, r, n):
        return remote(
            metric_ref.at[slab(0, x, n), pl.ds(0, width(hv))],
            metric.at[slab(g, x, n), pl.ds(0, width(hv))],
            m1_send.at[r, n], m1_recv.at[hv, n],
            (b, 2 * ((h + r) % pairs) + core),
        )

    def m3_own(hv):
        return remote(
            metric_ref.at[:, pl.ds(0, width(hv))], metric.at[rows(g), pl.ds(0, width(hv))],
            m3_send.at[hv], m3_recv.at[hv], (b, mate),
        )

    def m2_copy(hv, n):
        piece = metric.at[slab(2 * hv + core, x, n), pl.ds(0, width(hv))]
        return remote(piece, piece, m2_send.at[hv, n], m2_recv.at[hv, n], (across, g))

    def m3_copy(hv):
        piece = metric.at[rows(2 * hv + core), pl.ds(0, width(hv))]
        return remote(piece, piece, m3_send.at[hv], m3_recv.at[hv], (b, mate))

    for hv in range(pairs):
        @pl.when(h == hv)
        def _():
            for r in range(1, pairs):
                for n in range(parts):
                    m1_copy(hv, r, n).start()
            m3_own(hv).start()

    for c in order:
        @pl.when(jnp.logical_not(to_self(c)))
        def _():
            ints_copy(c).start()

        @pl.when(to_self(c))
        def _():
            pltpu.make_async_copy(ints_ref.at[c], ints.at[0, rows(g)], h_recv.at[g]).start()

    def z_copy(p):
        return remote(ints.at[0, rows(p)], ints.at[2, rows(p)], z_send.at[p], ring_recv.at[2, p], (ahead, g))

    def c_copy(p):
        return remote(ints.at[0, rows(p)], ints.at[1, rows(p)], c_send.at[p], ring_recv.at[1, p], (b, mate))

    def f_copy(p, role):
        return remote(ints.at[2, rows(p)], ints.at[role, rows(p)], f_send.at[p], ring_recv.at[role, p], (b, mate))

    def w_copy(p):
        return remote(ints.at[2, rows(p)], ints.at[3, rows(p)], w_send.at[p], ring_recv.at[3, p], (ahead, mate))

    def pass_own(p):
        landed(ints.at[0, rows(p)], h_recv.at[p])
        z_copy(p).start()

        @pl.when(core == 0)
        def _():
            c_copy(p).start()

    def pass_on(p):
        landed(ints.at[2, rows(p)], ring_recv.at[2, p])

        @pl.when(core == 1)
        def _():
            w_copy(p).start()
            f_copy(p, 1).start()

        @pl.when(core == 0)
        def _():
            f_copy(p, 3).start()

    for p in order[:2]:
        pass_own(p)
    for hv in range(pairs):
        @pl.when(h != hv)
        def _():
            for n in range(parts):
                landed(metric.at[slab(2 * hv + core, x, n), pl.ds(0, width(hv))], m1_recv.at[hv, n])
                m2_copy(hv, n).start()
    for p in order[:2]:
        pass_on(p)
    for hv in range(pairs):
        @pl.when(h != hv)
        def _():
            for n in range(parts):
                landed(metric.at[slab(2 * hv + core, 1 - x, n), pl.ds(0, width(hv))], m2_recv.at[hv, n])
            m3_copy(hv).start()
    for p in order[2:]:
        pass_own(p)

    own_metric.wait()
    for hv in range(pairs):
        landed(metric.at[rows(2 * hv + 1 - core), pl.ds(0, width(hv))], m3_recv.at[hv])

    levels = jnp.broadcast_to(vir_ref[...], (vir, vir))
    gap[...] = levels + levels.T

    def span(q):
        return pl.ds(pl.multiple_of(q * tile, tile), tile)

    @pl.loop(0, tiles)
    def _(p):
        @pl.loop(0, p + 1)
        def _(q):
            metric_t[span(q), span(p)] = metric[span(p), span(q)].T

    own_energy = occ_ref[own_b * groups + own_c]

    @pl.loop(0, CYCLE)
    def _(k):
        role = (k % 2) * 2 + k // 2

        @pl.when(k == 1)
        def _():
            for p in order[2:]:
                pass_on(p)

        @pl.when(role % 2 == 1)
        def _():
            for p in range(groups):
                landed(ints.at[role, rows(p)], ring_recv.at[role, p])

        for q in range(tiles):
            low = q * tile
            fit[low:low + tile, :] = jnp.dot(
                metric_t[low:low + tile, low:], ints[role, low:, :],
                preferred_element_type=jnp.float32,
            ).astype(fit.dtype)

        @pl.when(k == 0)
        def _():
            @pl.loop(0, tiles)
            def _(q):
                fit_t[:, span(q)] = fit[span(q), :].T

        pair = jnp.dot(fit_t[...], fit[...], preferred_element_type=jnp.float32)
        energy = own_energy + occ_ref[(own_b + blocks - role) % blocks * groups + own_c]
        amplitude_t = ((2.0 * pair.T - pair) / (energy - gap[...])).astype(fit.dtype)

        @pl.when(k == 0)
        def _():
            dens[...] = jnp.dot(fit[...], amplitude_t, preferred_element_type=jnp.float32)

        @pl.when((k > 0) & (k < CYCLE - 1))
        def _():
            dens[...] += jnp.dot(fit[...], amplitude_t, preferred_element_type=jnp.float32)

        @pl.when(k == CYCLE - 1)
        def _():
            total = dens[...] + jnp.dot(fit[...], amplitude_t, preferred_element_type=jnp.float32)
            dens_b[...] = total.astype(dens_b.dtype)

    def g_copy(p):
        return remote(gam.at[rows(p)], out_ref.at[own_c], g_send.at[p], g_recv.at[own_c], (own_b, p))

    def g_self(p):
        return (core == x) & (g == p)

    for t in range(tiles):
        low = t * tile
        gam[low:low + tile, :] = jnp.dot(
            metric[low:low + tile, :low + tile], dens_b[:low + tile, :],
            preferred_element_type=jnp.float32,
        ).astype(gam.dtype)
        for p in range(low // shard, (low + tile) // shard):
            @pl.when(jnp.logical_not(g_self(p)))
            def _():
                g_copy(p).start()

            @pl.when(g_self(p))
            def _():
                pltpu.make_async_copy(gam.at[rows(p)], out_ref.at[own_c], g_recv.at[own_c]).start()

    for c in range(groups):
        @pl.when(jnp.logical_not(to_self(c)))
        def _():
            ints_copy(c).wait_send()
        z_copy(c).wait_send()

        @pl.when(core == 0)
        def _():
            c_copy(c).wait_send()
        f_copy(c, 1).wait_send()

        @pl.when(core == 1)
        def _():
            w_copy(c).wait_send()

        @pl.when(jnp.logical_not(g_self(c)))
        def _():
            g_copy(c).wait_send()
    for hv in range(pairs):
        @pl.when(h == hv)
        def _():
            for r in range(1, pairs):
                for n in range(parts):
                    m1_copy(hv, r, n).wait_send()
            m3_own(hv).wait_send()

        @pl.when(h != hv)
        def _():
            for n in range(parts):
                m2_copy(hv, n).wait_send()
            m3_copy(hv).wait_send()
    for c in range(groups):
        landed(out_ref.at[c], g_recv.at[c])


def local(half_ints, metric_inv, occ_energy, vir_energy):
    groups, blocks = lax.axis_size("aux"), lax.axis_size("blk")
    shard, vir = half_ints.shape[1:]
    naux = metric_inv.shape[1]
    tile = shard if shard % 128 == 0 else naux // 4
    pairs = groups // 2
    parts = 4 if shard % 128 == 0 else 1
    dma = pltpu.SemaphoreType.DMA
    return pl.pallas_call(
        functools.partial(kernel, blocks, groups, tile),
        out_shape=jax.ShapeDtypeStruct(half_ints.shape, jnp.bfloat16),
        in_specs=[
            pl.BlockSpec(memory_space=pl.ANY),
            pl.BlockSpec(memory_space=pl.ANY),
            pl.BlockSpec(memory_space=pltpu.SMEM),
            pl.BlockSpec(memory_space=pltpu.VMEM),
        ],
        out_specs=pl.BlockSpec(memory_space=pl.ANY),
        scratch_shapes=[
            pltpu.VMEM((CYCLE, naux, vir), jnp.bfloat16),
            pltpu.VMEM((naux, naux), jnp.bfloat16),
            pltpu.VMEM((naux, naux), jnp.bfloat16),
            pltpu.VMEM((naux, vir), jnp.bfloat16),
            pltpu.VMEM((vir, naux), jnp.bfloat16),
            pltpu.VMEM((vir, vir), jnp.float32),
            pltpu.VMEM((naux, vir), jnp.float32),
            pltpu.VMEM((naux, vir), jnp.bfloat16),
            pltpu.VMEM((naux, vir), jnp.bfloat16),
            dma((groups,)), dma((groups,)), dma((groups,)), dma((groups,)), dma((groups,)),
            dma((groups,)), dma((CYCLE, groups)),
            dma((pairs, parts)), dma((pairs, parts)), dma((pairs, parts)), dma((pairs, parts)), dma((pairs,)), dma((pairs,)),
            dma(()), dma((groups,)), dma((groups,)),
        ],
        compiler_params=pltpu.CompilerParams(
            collective_id=0, has_side_effects=True, vmem_limit_bytes=56 * 2**20
        ),
    )(half_ints, metric_inv, occ_energy, vir_energy)


def solution(mesh):
    placed = (P("blk", "aux", None), P("aux", None), P(), P())
    return jax.shard_map(
        local, mesh=mesh, in_specs=placed, out_specs=P("blk", "aux", None), check_vma=False
    )
```
